32 devices in a mesh: fsdp: 4 (over z), ctx: 2 (over y), tp: 4 (over x, core).
Axes of the slice: x: 2, y: 2, z: 4, core: 2. Of those that a mesh axis runs over, the one named last changes fastest.
Arguments:
- block_input: bfloat16 [8, 2048, 1024], P('fsdp', 'ctx', 'tp'), may hold values from -45 to 45
- positions: int32 [8, 2048], P('fsdp', 'ctx'), may hold values from 0 to 2047, as said below
- first_gain: bfloat16 [1024], P('fsdp'), may hold values from 0.5 to 1.5
- first_shift: bfloat16 [1024], P('fsdp'), may hold values from -3 to 3
- second_gain: bfloat16 [1024], P('fsdp'), may hold values from 0.5 to 1.5
- second_shift: bfloat16 [1024], P('fsdp'), may hold values from -3 to 3
- triple_weight: bfloat16 [1024, 3, 1024], P('fsdp', None, 'tp'), as said below
- triple_bias: bfloat16 [3, 16, 64], P(None, 'tp', 'fsdp'), may hold values from -64 to 64
- mixer_weight: bfloat16 [1024, 1024], P('tp', 'fsdp'), may hold values from -2 to 2
- output_bias: bfloat16 [1024], P('fsdp'), may hold values from -3 to 3
- widen_weight: bfloat16 [1024, 4096], P('fsdp', 'tp'), may hold values from -0.1875 to 0.1875
- widen_bias: bfloat16 [32, 128], P('tp', 'fsdp'), may hold values from -3 to 3
- narrow_weight: bfloat16 [4096, 1024], P('tp', 'fsdp'), may hold values from -0.09375 to 0.09375
- cotangent: bfloat16 [8, 2048, 1024], P('fsdp', 'ctx', 'tp'), may hold values from -6 to 6
Outputs:
- block_output: bfloat16 [8, 2048, 1024], P('fsdp', 'ctx', 'tp')
- input_grad: bfloat16 [8, 2048, 1024], P('fsdp', 'ctx', 'tp')
- first_gain_grad: float32 [1024], P('fsdp')
- first_shift_grad: float32 [1024], P('fsdp')
- second_gain_grad: float32 [1024], P('fsdp')
- second_shift_grad: float32 [1024], P('fsdp')
- triple_weight_grad: float32 [1024, 3, 1024], P('fsdp', None, 'tp')
- triple_bias_grad: float32 [3, 16, 64], P(None, 'tp', 'fsdp')
- mixer_weight_grad: float32 [1024, 1024], P('tp', 'fsdp')
- output_bias_grad: float32 [1024], P('fsdp')
- widen_weight_grad: float32 [1024, 4096], P('fsdp', 'tp')
- widen_bias_grad: float32 [32, 128], P('tp', 'fsdp')
- narrow_weight_grad: float32 [4096, 1024], P('tp', 'fsdp')
The draws below stay inside these ranges and needn't reach their ends.
Inputs may be any that keep to these rules, and one draw needn't show every extreme that they name: `positions`: each row counts up by one from 0 and falls back to 0 where a packed document begins; a row holds at most four documents; the first sequence is one whole document. `triple_weight`: entries are at most 4 / sqrt(1024) in magnitude.
All inputs are finite; a program needn't handle non-finite values.
Results may differ from the reference program's by a relative error of at most 0.017.
Values may be sent and summed in bfloat16 or wider, within the bound.
A program may use at most 192 MiB of HBM per device.

```python
import math
import jax
import jax.numpy as jnp
from jax import lax

D = 1024
H = 16
HD = 64
ROT = 16
FF = 4096
LEN = 2048
SEQS = 8


def draw_block_input(key, part):
    noise_key = jax.random.fold_in(key, 0)
    values = jax.random.truncated_normal(noise_key, -5.0, 5.0, (SEQS, LEN, D), jnp.float32)
    return values.astype(jnp.bfloat16)


def draw_positions(key, part):
    cuts = jax.random.randint(key, (SEQS, 3, 1), 1, LEN, dtype=jnp.int32)
    whole = (jnp.arange(SEQS, dtype=jnp.int32) == 0)[:, None, None]
    cuts = jnp.where(whole, jnp.int32(LEN), cuts)
    index = jnp.arange(LEN, dtype=jnp.int32)
    starts = jnp.max(jnp.where(cuts <= index, cuts, 0), axis=1)
    return (index[None, :] - starts).astype(jnp.int32)


def draw_triple_weight(key, part):
    base_key = jax.random.fold_in(key, 3)
    values = jax.random.truncated_normal(base_key, -4.0, 4.0, (D, 3, D), jnp.float32)
    return (values * (1.0 / math.sqrt(D))).astype(jnp.bfloat16)


def draw_triple_bias(key, part):
    base_key = jax.random.fold_in(key, 5)
    values = jax.random.truncated_normal(base_key, -4.0, 4.0, (3, H, HD), jnp.float32) * 0.1
    return values.astype(jnp.bfloat16)


def strengthened(entries, own_key, source, target, parts, factor):
    owner, partner = [(jnp.arange(entries.shape[position]) // (entries.shape[position] // parts)).reshape([-1 if axis == position else 1 for axis in range(entries.ndim)]) for position in (source, target)]
    chosen = jax.random.permutation(own_key, parts)[partner]
    strong = (owner == chosen) | (owner == (partner + parts // 2) % parts)
    return jnp.where(strong, factor * entries, entries)


def steps_of(rng, dims, cuts, low, top_value):
    loudness = 1.0
    for axis_at, shards_of in cuts:
        heights = jax.random.uniform(jax.random.fold_in(jax.random.fold_in(rng, 6), axis_at), (shards_of,), jnp.float32, low / len(cuts), top_value / len(cuts))
        loudness = loudness * jnp.repeat(jnp.exp(heights), dims[axis_at] // shards_of).reshape((-1,) + (1,) * (len(dims) - 1 - axis_at))
    return loudness


def gaussian(own_key, extent, width, most, cuts=(), kind=jnp.bfloat16):
    result = width * jax.random.normal(own_key, extent, jnp.float32)
    if cuts:
        result = result * steps_of(own_key, extent, cuts, -0.22, 0.18)
    return jnp.clip(result, -most, most).astype(kind)


def noise_with(own_key, shape, spread, limit, shards, heavy, held_as=jnp.bfloat16):
    values = spread * jax.random.normal(own_key, shape, jnp.float32)
    if shards:
        values = values * steps_of(own_key, shape, shards, -0.22, 0.18)
    return jnp.clip(strengthened(values, jax.random.fold_in(own_key, 3), *heavy), -limit, limit).astype(held_as)


def setup_inputs(seed: int = 0) -> dict:
    streams_of = jax.random.split(jax.random.key(seed), 15)
    block_input = draw_block_input(jax.random.fold_in(streams_of[14], 71), 0)
    positions = draw_positions(jax.random.fold_in(streams_of[14], 71), 0)
    first_gain = jnp.clip(1.0 + 0.1 * jax.random.normal(streams_of[2], (D,), jnp.float32), 0.5, 1.5).astype(jnp.bfloat16)
    first_shift = gaussian(streams_of[3], (D,), 0.3, 3.0, ((0, 4),))
    second_gain = jnp.clip(1.0 + 0.1 * jax.random.normal(streams_of[4], (D,), jnp.float32), 0.5, 1.5).astype(jnp.bfloat16)
    second_shift = gaussian(streams_of[5], (D,), 0.3, 3.0, ((0, 4),))
    triple_weight = draw_triple_weight(jax.random.fold_in(streams_of[14], 71), 0)
    triple_bias = draw_triple_bias(jax.random.fold_in(streams_of[14], 71), 0)
    mixer_weight = gaussian(streams_of[8], (D, D), (HD // 8) ** -0.5, 2.0, ((0, 4), (1, 4)))
    output_bias = gaussian(streams_of[9], (D,), 0.3, 3.0, ((0, 4),))
    widen_weight = gaussian(streams_of[10], (D, FF), D ** -0.5, 0.1875, ((0, 4), (1, 4)))
    widen_bias = gaussian(streams_of[11], (FF // 128, 128), 0.5, 3.0, ((0, 4), (1, 4)))
    narrow_weight = gaussian(streams_of[12], (FF, D), FF ** -0.5, 0.09375, ((0, 4), (1, 4)))
    cotangent = noise_with(streams_of[13], (SEQS, LEN, D), 1.0, 6.0, ((0, 4), (1, 2), (2, 4)), (0, 2, 4, 2.0))
    return {"block_input": block_input, "positions": positions, "first_gain": first_gain, "first_shift": first_shift, "second_gain": second_gain, "second_shift": second_shift, "triple_weight": triple_weight, "triple_bias": triple_bias, "mixer_weight": mixer_weight, "output_bias": output_bias, "widen_weight": widen_weight, "widen_bias": widen_bias, "narrow_weight": narrow_weight, "cotangent": cotangent}


norm_eps = 1e-05
masked_score = -1e+30

def normalize(rows):
    centred = rows - lax.optimization_barrier(jnp.mean(rows, axis=-1, keepdims=True))
    inverse = lax.rsqrt(lax.optimization_barrier(jnp.mean(centred * centred, axis=-1, keepdims=True)) + norm_eps)
    return (centred * inverse, inverse)

def gelu_parts(widened):
    cumulative = 0.5 * (1.0 + lax.erf(widened * (1.0 / math.sqrt(2.0))))
    density = jnp.exp(-0.5 * widened * widened) * (1.0 / math.sqrt(2.0 * math.pi))
    return (widened * cumulative, cumulative + widened * density)

def rotate_forward(block, cosine, sine, half):
    first = block[..., :half]
    second = block[..., half:2 * half]
    return jnp.concatenate([first * cosine - second * sine, second * cosine + first * sine, block[..., 2 * half:]], axis=-1)

def rotate_back(block, cosine, sine, half):
    first = block[..., :half]
    second = block[..., half:2 * half]
    return jnp.concatenate([first * cosine + second * sine, second * cosine - first * sine, block[..., 2 * half:]], axis=-1)

def norm_back(grad, gain, normed, inverse):
    scaled = grad * gain
    return inverse * (scaled - lax.optimization_barrier(jnp.mean(scaled, axis=-1, keepdims=True)) - normed * lax.optimization_barrier(jnp.mean(scaled * normed, axis=-1, keepdims=True)))

def reference(block_input, positions, first_gain, first_shift, second_gain, second_shift, triple_weight, triple_bias, mixer_weight, output_bias, widen_weight, widen_bias, narrow_weight, cotangent):
    scale = HD ** (-0.5)
    half = ROT // 2
    gain_first = first_gain.astype(jnp.float32)
    shift_first = first_shift.astype(jnp.float32)
    gain_second = second_gain.astype(jnp.float32)
    shift_second = second_shift.astype(jnp.float32)
    flat_triple = triple_weight.reshape(D, 3 * D)
    bias_triple = triple_bias.astype(jnp.float32)
    bias_widen = widen_bias.reshape(FF).astype(jnp.float32)
    bias_output = output_bias.astype(jnp.float32)
    index = jnp.arange(LEN, dtype=jnp.int32)
    freqs = jnp.exp(jnp.arange(half, dtype=jnp.float32) * (-2.0 * math.log(10000.0) / ROT))

    def one_sequence(totals, inputs):
        rows_in, places, cot_rows = inputs
        normed, inverse = normalize(rows_in.astype(jnp.float32))
        first_rows = (normed * gain_first + shift_first).astype(jnp.bfloat16)
        second_rows = (normed * gain_second + shift_second).astype(jnp.bfloat16)
        projected = jnp.dot(first_rows, flat_triple, preferred_element_type=jnp.float32).reshape(LEN, 3, H, HD) + bias_triple
        angles = places.astype(jnp.float32)[:, None] * freqs[None, :]
        cosine = jnp.cos(angles)[:, None, None, :]
        sine = jnp.sin(angles)[:, None, None, :]
        turned = rotate_forward(projected[:, :2], cosine, sine, half)
        triple = jnp.concatenate([turned, projected[:, 2:]], axis=1).astype(jnp.bfloat16)
        by_heads = jnp.transpose(triple, (1, 2, 0, 3))
        visible = (index[None, :] <= index[:, None]) & (places[:, None] - places[None, :] == index[:, None] - index[None, :])

        def head_scores(queries, keys_in):
            scores = jnp.dot(queries, keys_in.T, preferred_element_type=jnp.float32) * scale
            return jnp.where(visible, scores, masked_score)

        def head_forward(args):
            queries, keys_in, values_in = args
            scores = head_scores(queries, keys_in)
            top = lax.optimization_barrier(jnp.max(scores, axis=1, keepdims=True))
            logsum = top + jnp.log(lax.optimization_barrier(jnp.sum(jnp.exp(scores - top), axis=1, keepdims=True)))
            weights = jnp.exp(scores - logsum).astype(jnp.bfloat16)
            mixed = jnp.dot(weights, values_in, preferred_element_type=jnp.float32).astype(jnp.bfloat16)
            return (mixed, logsum[:, 0])

        def head_backward(args):
            queries, keys_in, values_in, mixed, logsum, grad_mixed = args
            scores = head_scores(queries, keys_in)
            probs = jnp.exp(scores - logsum[:, None])
            values_grad = jnp.dot(probs.astype(jnp.bfloat16).T, grad_mixed, preferred_element_type=jnp.float32).astype(jnp.bfloat16)
            prob_grads = jnp.dot(grad_mixed, values_in.T, preferred_element_type=jnp.float32)
            delta = lax.optimization_barrier(jnp.sum(grad_mixed.astype(jnp.float32) * mixed.astype(jnp.float32), axis=1))
            score_grads = (probs * (prob_grads - delta[:, None])).astype(jnp.bfloat16)
            queries_grad = (jnp.dot(score_grads, keys_in, preferred_element_type=jnp.float32) * scale).astype(jnp.bfloat16)
            keys_grad = (jnp.dot(score_grads.T, queries, preferred_element_type=jnp.float32) * scale).astype(jnp.bfloat16)
            return (queries_grad, keys_grad, values_grad)
        mixed, logsum = lax.map(head_forward, (by_heads[0], by_heads[1], by_heads[2]))
        mixed_rows = jnp.transpose(mixed, (1, 0, 2)).reshape(LEN, D)
        widened = jnp.dot(second_rows, widen_weight, preferred_element_type=jnp.float32) + bias_widen
        activated_float, slope = gelu_parts(widened)
        activated = activated_float.astype(jnp.bfloat16)
        branches = jnp.dot(mixed_rows, mixer_weight, preferred_element_type=jnp.float32) + jnp.dot(activated, narrow_weight, preferred_element_type=jnp.float32)
        block_output = (rows_in.astype(jnp.float32) + branches + bias_output).astype(jnp.bfloat16)
        output_bias_grad = lax.optimization_barrier(jnp.sum(cot_rows.astype(jnp.float32), axis=0))
        narrow_grad = jnp.dot(activated.T, cot_rows, preferred_element_type=jnp.float32)
        hidden_grad = jnp.dot(cot_rows, narrow_weight.T, preferred_element_type=jnp.float32) * slope
        widen_bias_grad = lax.optimization_barrier(jnp.sum(hidden_grad, axis=0))
        hidden_rounded = hidden_grad.astype(jnp.bfloat16)
        widen_grad = jnp.dot(second_rows.T, hidden_rounded, preferred_element_type=jnp.float32)
        second_grad = jnp.dot(hidden_rounded, widen_weight.T, preferred_element_type=jnp.float32)
        mixer_grad = jnp.dot(mixed_rows.T, cot_rows, preferred_element_type=jnp.float32)
        mixed_grad = jnp.dot(cot_rows, mixer_weight.T, preferred_element_type=jnp.float32).astype(jnp.bfloat16)
        mixed_grad = jnp.transpose(mixed_grad.reshape(LEN, H, HD), (1, 0, 2))
        queries_grad, keys_grad, values_grad = lax.map(head_backward, (by_heads[0], by_heads[1], by_heads[2], mixed, logsum, mixed_grad))
        back = jnp.transpose(jnp.stack([queries_grad, keys_grad, values_grad], axis=0), (2, 0, 1, 3)).astype(jnp.float32)
        unturned = rotate_back(back[:, :2], cosine, sine, half)
        projected_grad = jnp.concatenate([unturned, back[:, 2:]], axis=1)
        triple_bias_grad = lax.optimization_barrier(jnp.sum(projected_grad, axis=0))
        projected_rounded = projected_grad.astype(jnp.bfloat16).reshape(LEN, 3 * D)
        triple_grad = jnp.dot(first_rows.T, projected_rounded, preferred_element_type=jnp.float32).reshape(D, 3, D)
        first_grad = jnp.dot(projected_rounded, flat_triple.T, preferred_element_type=jnp.float32)
        first_gain_grad = lax.optimization_barrier(jnp.sum(first_grad * normed, axis=0))
        first_shift_grad = lax.optimization_barrier(jnp.sum(first_grad, axis=0))
        second_gain_grad = lax.optimization_barrier(jnp.sum(second_grad * normed, axis=0))
        second_shift_grad = lax.optimization_barrier(jnp.sum(second_grad, axis=0))
        rows_grad = cot_rows.astype(jnp.float32) + norm_back(first_grad, gain_first, normed, inverse) + norm_back(second_grad, gain_second, normed, inverse)
        input_grad = rows_grad.astype(jnp.bfloat16)
        terms = (first_gain_grad, first_shift_grad, second_gain_grad, second_shift_grad, triple_grad, triple_bias_grad, mixer_grad, output_bias_grad, widen_grad, widen_bias_grad, narrow_grad)
        totals = tuple((total + term for total, term in zip(totals, terms)))
        return (totals, (block_output, input_grad))
    zeros = (jnp.zeros((D,), jnp.float32), jnp.zeros((D,), jnp.float32), jnp.zeros((D,), jnp.float32), jnp.zeros((D,), jnp.float32), jnp.zeros((D, 3, D), jnp.float32), jnp.zeros((3, H, HD), jnp.float32), jnp.zeros((D, D), jnp.float32), jnp.zeros((D,), jnp.float32), jnp.zeros((D, FF), jnp.float32), jnp.zeros((FF,), jnp.float32), jnp.zeros((FF, D), jnp.float32))
    totals, (block_output, input_grad) = lax.scan(one_sequence, zeros, (block_input, positions, cotangent))
    return (block_output, input_grad, totals[0], totals[1], totals[2], totals[3], totals[4], totals[5], totals[6], totals[7], totals[8], totals[9].reshape(FF // 128, 128), totals[10])
```

```python
import functools
import math

import jax
import jax.numpy as jnp
from jax import lax
from jax.experimental import pallas as pl
from jax.experimental.pallas import tpu as pltpu
from jax.sharding import PartitionSpec as P

ROT = 16


norm_eps = 1e-05
masked_score = -1e30


def normalize(rows):
    centred = rows - jnp.mean(rows, axis=-1, keepdims=True)
    inverse = lax.rsqrt(jnp.mean(centred * centred, axis=-1, keepdims=True) + norm_eps)
    return (centred * inverse, inverse)


def gelu_parts(widened):
    cumulative = 0.5 * (1.0 + lax.erf(widened * (1.0 / math.sqrt(2.0))))
    density = jnp.exp(-0.5 * widened * widened) * (1.0 / math.sqrt(2.0 * math.pi))
    return (widened * cumulative, cumulative + widened * density)


def rotary_tables(positions, rotary):
    half = rotary // 2
    freqs = jnp.exp(jnp.arange(half, dtype=jnp.float32) * (-2.0 * math.log(10000.0) / rotary))
    angles = positions.astype(jnp.float32)[:, None, :] * freqs[None, :, None]
    return (jnp.cos(angles)[:, None, None], jnp.sin(angles)[:, None, None])


def rotate_forward(block, cosine, sine, half):
    first = block[..., :half, :]
    second = block[..., half : 2 * half, :]
    return jnp.concatenate(
        [first * cosine - second * sine, second * cosine + first * sine, block[..., 2 * half :, :]],
        axis=-2,
    )


def rotate_back(block, cosine, sine, half):
    first = block[..., :half, :]
    second = block[..., half : 2 * half, :]
    return jnp.concatenate(
        [first * cosine + second * sine, second * cosine - first * sine, block[..., 2 * half :, :]],
        axis=-2,
    )


def attend_kernel(block, scale, qkv_ref, grad_ref, base_ref, back_ref, mixed_ref,
                  queries, query_rows, keys, key_rows, values, value_rows, grads, grad_rows,
                  base_rows, key_sum, value_sum):
    parts, head_size, span = grad_ref.shape[0], grad_ref.shape[2], grad_ref.shape[3]
    length = parts * span
    for part in range(parts):
        at = pl.ds(part * span, span)
        queries[:, at] = (qkv_ref[part, 0, 0].astype(jnp.float32) * scale).astype(jnp.bfloat16)
        keys[:, at] = qkv_ref[part, 0, 1]
        values[:, at] = qkv_ref[part, 0, 2]
        grads[:, at] = grad_ref[part, 0]
    for source, target in (
        (queries, query_rows),
        (keys, key_rows),
        (values, value_rows),
        (grads, grad_rows),
    ):
        target[...] = source[...].astype(jnp.float32).T.astype(jnp.bfloat16)
    base_row = base_ref[0]
    base_rows[...] = jnp.broadcast_to(base_row, (128, length)).T
    for start in range(0, length, block):
        count = start + block
        here = slice(start, count)
        scores = jnp.dot(key_rows[:count], queries[:, here], preferred_element_type=jnp.float32)
        wide_base = jnp.concatenate([base_rows[:count]] * (block // 128), axis=1)
        same = wide_base == base_row[:, here]
        key_index = lax.broadcasted_iota(jnp.int32, (block, block), 0)
        query_index = lax.broadcasted_iota(jnp.int32, (block, block), 1)
        last = jnp.where(
            same[start:] & (key_index <= query_index), scores[start:], masked_score
        )
        if start:
            earlier = jnp.where(same[:start], scores[:start], masked_score)
            scores = jnp.concatenate([earlier, last], axis=0)
        else:
            scores = last
        top = jnp.max(scores, axis=0, keepdims=True)
        raised = jnp.exp(scores - top)
        probs = raised * (1.0 / jnp.sum(raised, axis=0, keepdims=True))
        weights = probs.astype(jnp.bfloat16)
        mixed = jnp.dot(values[:, :count], weights, preferred_element_type=jnp.float32).astype(
            jnp.bfloat16
        )
        grad_block = grads[:, here]
        delta = jnp.sum(
            mixed.astype(jnp.float32) * grad_block.astype(jnp.float32), axis=0, keepdims=True
        )
        prob_grads = jnp.dot(value_rows[:count], grad_block, preferred_element_type=jnp.float32)
        score_grads = (probs * (prob_grads - delta)).astype(jnp.bfloat16)
        query_part = jnp.dot(keys[:, :count], score_grads, preferred_element_type=jnp.float32)
        key_part = jnp.dot(score_grads, query_rows[here], preferred_element_type=jnp.float32)
        value_part = jnp.dot(weights, grad_rows[here], preferred_element_type=jnp.float32)
        if start:
            key_sum[:start] += key_part[:start]
            value_sum[:start] += value_part[:start]
        key_sum[here] = key_part[start:]
        value_sum[here] = value_part[start:]
        part, inside = start // span, start % span
        mixed_ref[part, 0, :, inside : inside + block] = mixed
        back_ref[part, 0, 0, :, inside : inside + block] = (query_part * scale).astype(jnp.bfloat16)
    for part in range(parts):
        at = pl.ds(part * span, span)
        back_ref[part, 0, 1] = key_sum[at].T.astype(jnp.bfloat16)
        back_ref[part, 0, 2] = value_sum[at].T.astype(jnp.bfloat16)


def attend(by_heads, grad_heads, item_base, scale):
    parts, items, unused, head_size, span = by_heads.shape
    length = parts * span
    block = min(256, span)
    wide = pltpu.VMEM((head_size, length), jnp.bfloat16)
    tall = pltpu.VMEM((length, head_size), jnp.bfloat16)
    total = pltpu.VMEM((length, head_size), jnp.float32)
    return pl.pallas_call(
        functools.partial(attend_kernel, block, scale),
        grid=(items,),
        in_specs=[
            pl.BlockSpec((parts, 1, 3, head_size, span), lambda i: (0, i, 0, 0, 0)),
            pl.BlockSpec((parts, 1, head_size, span), lambda i: (0, i, 0, 0)),
            pl.BlockSpec((1, 1, length), lambda i: (i, 0, 0)),
        ],
        out_specs=[
            pl.BlockSpec((parts, 1, 3, head_size, span), lambda i: (0, i, 0, 0, 0)),
            pl.BlockSpec((parts, 1, head_size, span), lambda i: (0, i, 0, 0)),
        ],
        out_shape=[
            jax.ShapeDtypeStruct(by_heads.shape, jnp.bfloat16),
            jax.ShapeDtypeStruct(grad_heads.shape, jnp.bfloat16),
        ],
        scratch_shapes=[wide, tall, wide, tall, wide, tall, wide, tall,
                        pltpu.VMEM((length, 128), jnp.float32), total, total],
        compiler_params=pltpu.CompilerParams(vmem_limit_bytes=48 * 1024 * 1024),
        cost_estimate=pl.CostEstimate(
            flops=7 * items * length * length * 256,
            bytes_accessed=4 * by_heads.size,
            transcendentals=items * length * length // 2,
        ),
    )(by_heads, grad_heads, item_base)


def sum_pair(share, axis):
    size = lax.axis_size(axis)
    if size == 2:
        other = lax.ppermute(share, axis, [(0, 1), (1, 0)])
        return share.astype(jnp.float32) + other.astype(jnp.float32)
    return lax.psum(share, axis).astype(jnp.float32)


def shards(
    block_input,
    positions,
    first_gain,
    first_shift,
    second_gain,
    second_shift,
    triple_weight,
    triple_bias,
    mixer_weight,
    output_bias,
    widen_weight,
    widen_bias,
    narrow_weight,
    cotangent,
):
    seqs, local_tokens, local_width = block_input.shape
    vectors = (first_gain, first_shift, second_gain, second_shift, output_bias, triple_bias, widen_bias)
    small = lax.all_gather(
        jnp.concatenate([vector.reshape(-1) for vector in vectors]), "fsdp", axis=0, tiled=False
    )
    groups = small.shape[0]
    pieces = []
    offset = 0
    for vector in vectors:
        pieces.append(small[:, offset : offset + vector.size].astype(jnp.float32))
        offset += vector.size
    gain_one, shift_one, gain_two, shift_two, bias_output = [
        piece.reshape(-1) for piece in pieces[:5]
    ]
    bias_triple = jnp.transpose(
        pieces[5].reshape((groups,) + triple_bias.shape), (1, 2, 0, 3)
    ).reshape(triple_bias.shape[0], triple_bias.shape[1], -1)
    bias_widen = jnp.transpose(
        pieces[6].reshape((groups,) + widen_bias.shape), (1, 0, 2)
    ).reshape(-1)
    all_positions = lax.all_gather(positions, "ctx", axis=1, tiled=True)
    whole_input = lax.all_gather(block_input, "tp", axis=2, tiled=True)
    weight_triple = lax.all_gather(triple_weight, "fsdp", axis=0, tiled=True)
    whole_cot = lax.all_gather(cotangent, "tp", axis=2, tiled=True)
    mixer_rows = mixer_weight.shape[0]
    joined = lax.all_gather(
        jnp.concatenate([mixer_weight, narrow_weight], axis=0), "fsdp", axis=1, tiled=True
    )
    weight_mixer, weight_narrow = joined[:mixer_rows], joined[mixer_rows:]
    weight_widen = lax.all_gather(widen_weight, "fsdp", axis=0, tiled=True)
    width = weight_triple.shape[0]
    heads_local, head_size = bias_triple.shape[1:]
    feature_start = lax.axis_index("tp") * local_width
    scale = head_size ** (-0.5)
    half = ROT // 2
    normed, inverse = normalize(whole_input.astype(jnp.float32))
    first_rows = (normed * gain_one + shift_one).astype(jnp.bfloat16)
    second_rows = (normed * gain_two + shift_two).astype(jnp.bfloat16)
    cosine, sine = rotary_tables(positions, ROT)
    weight_four = weight_triple.reshape(width, 3, heads_local, head_size)
    projected = jnp.einsum(
        "std,dchk->shckt", first_rows, weight_four, preferred_element_type=jnp.float32
    )
    projected = projected + jnp.transpose(bias_triple, (1, 0, 2))[None, :, :, :, None]
    turned = rotate_forward(projected[:, :, :2], cosine, sine, half)
    triple = jnp.concatenate([turned, projected[:, :, 2:]], axis=2).astype(jnp.bfloat16)
    parts = lax.axis_size("ctx")
    items = seqs * heads_local // parts
    by_heads = lax.all_to_all(
        triple.reshape(parts, items, 3, head_size, local_tokens),
        "ctx",
        split_axis=0,
        concat_axis=0,
        tiled=True,
    )
    mixer_four = weight_mixer.reshape(heads_local, head_size, width)
    mixed_grad = jnp.einsum(
        "ste,hke->shkt", whole_cot, mixer_four, preferred_element_type=jnp.float32
    ).astype(jnp.bfloat16)
    grad_heads = lax.all_to_all(
        mixed_grad.reshape(parts, items, head_size, local_tokens),
        "ctx",
        split_axis=0,
        concat_axis=0,
        tiled=True,
    )
    length = all_positions.shape[1]
    item_seq = (lax.axis_index("ctx") * items + jnp.arange(items, dtype=jnp.int32)) // heads_local
    base = (jnp.arange(length, dtype=jnp.int32)[None, :] - all_positions).astype(jnp.float32)
    item_base = jnp.take(base, item_seq, axis=0)[:, None, :]
    back_heads, mixed = attend(by_heads, grad_heads, item_base, scale)
    mixed_tokens = lax.all_to_all(
        mixed, "ctx", split_axis=0, concat_axis=0, tiled=True
    ).reshape(seqs, heads_local, head_size, local_tokens)
    back_float = (
        lax.all_to_all(back_heads, "ctx", split_axis=0, concat_axis=0, tiled=True)
        .reshape(seqs, heads_local, 3, head_size, local_tokens)
        .astype(jnp.float32)
    )
    widened = (
        jnp.einsum("std,df->stf", second_rows, weight_widen, preferred_element_type=jnp.float32)
        + bias_widen
    )
    activated_float, slope = gelu_parts(widened)
    activated = activated_float.astype(jnp.bfloat16)
    hidden_grad = (
        jnp.einsum("ste,fe->stf", whole_cot, weight_narrow, preferred_element_type=jnp.float32)
        * slope
    )
    widen_bias_grad = jnp.sum(hidden_grad, axis=(0, 1))
    hidden_rounded = hidden_grad.astype(jnp.bfloat16)
    narrow_grad = jnp.einsum(
        "stf,ste->fe", activated, whole_cot, preferred_element_type=jnp.float32
    ).astype(jnp.bfloat16)
    narrow_share = lax.psum_scatter(narrow_grad, "fsdp", scatter_dimension=1, tiled=True)
    widen_grad = jnp.einsum(
        "std,stf->df", second_rows, hidden_rounded, preferred_element_type=jnp.float32
    ).astype(jnp.bfloat16)
    widen_share = lax.psum_scatter(widen_grad, "fsdp", scatter_dimension=0, tiled=True)
    second_grad = jnp.einsum(
        "stf,df->std", hidden_rounded, weight_widen, preferred_element_type=jnp.float32
    ).astype(jnp.bfloat16)
    attention_part = jnp.einsum(
        "shkt,hke->ste", mixed_tokens, mixer_four, preferred_element_type=jnp.float32
    )
    branches = attention_part + jnp.einsum(
        "stf,fe->ste", activated, weight_narrow, preferred_element_type=jnp.float32
    )
    summed = lax.psum_scatter(
        branches.astype(jnp.bfloat16), "tp", scatter_dimension=2, tiled=True
    ).astype(jnp.float32)
    bias_slice = lax.dynamic_slice_in_dim(bias_output, feature_start, local_width, 0)
    block_output = (block_input.astype(jnp.float32) + summed + bias_slice).astype(jnp.bfloat16)
    mixer_grad = (
        jnp.einsum("shkt,ste->hke", mixed_tokens, whole_cot, preferred_element_type=jnp.float32)
        .reshape(weight_mixer.shape)
        .astype(jnp.bfloat16)
    )
    mixer_share = lax.psum_scatter(mixer_grad, "fsdp", scatter_dimension=1, tiled=True)
    unturned = rotate_back(back_float[:, :, :2], cosine, sine, half)
    projected_grad = jnp.concatenate([unturned, back_float[:, :, 2:]], axis=2)
    triple_bias_grad = jnp.transpose(jnp.sum(projected_grad, axis=(0, 4)), (1, 0, 2))
    projected_rounded = projected_grad.astype(jnp.bfloat16)
    first_grad = jnp.einsum(
        "shckt,dchk->std", projected_rounded, weight_four, preferred_element_type=jnp.float32
    ).astype(jnp.bfloat16)
    first_float = first_grad.astype(jnp.float32)
    second_float = second_grad.astype(jnp.float32)
    scaled = first_float * gain_one + second_float * gain_two
    scattered = lax.psum_scatter(
        scaled.astype(jnp.bfloat16), "tp", scatter_dimension=2, tiled=True
    ).astype(jnp.float32)
    row_sums = lax.psum(
        jnp.stack([jnp.sum(scaled, axis=-1), jnp.sum(scaled * normed, axis=-1)]), "tp"
    ) * (1.0 / width)
    triple_grad = (
        jnp.einsum(
            "std,shckt->dchk", first_rows, projected_rounded, preferred_element_type=jnp.float32
        )
        .reshape(weight_triple.shape)
        .astype(jnp.bfloat16)
    )
    triple_share = lax.psum_scatter(triple_grad, "fsdp", scatter_dimension=0, tiled=True)
    output_bias_grad = jnp.sum(whole_cot.astype(jnp.float32), axis=(0, 1))
    wide_sums = jnp.stack(
        [
            jnp.sum(first_float * normed, axis=(0, 1)),
            jnp.sum(first_float, axis=(0, 1)),
            jnp.sum(second_float * normed, axis=(0, 1)),
            jnp.sum(second_float, axis=(0, 1)),
            jnp.where(lax.axis_index("tp") == 0, output_bias_grad, 0.0),
        ]
    )
    wide_sums = lax.psum(wide_sums, ("fsdp", "ctx", "tp"))
    bias_sums = lax.psum(
        jnp.concatenate([triple_bias_grad.reshape(-1), widen_bias_grad]), ("fsdp", "ctx")
    )
    place = lax.axis_index("fsdp")
    vector_size = first_gain.shape[0]
    wide_sums = lax.dynamic_slice_in_dim(wide_sums, place * vector_size, vector_size, 1)
    triple_bias_out = lax.dynamic_slice_in_dim(
        bias_sums[: triple_bias_grad.size].reshape(triple_bias_grad.shape),
        place * triple_bias.shape[2],
        triple_bias.shape[2],
        2,
    )
    widen_bias_out = lax.dynamic_slice_in_dim(
        bias_sums[triple_bias_grad.size :].reshape(widen_bias.shape[0], -1),
        place * widen_bias.shape[1],
        widen_bias.shape[1],
        1,
    )
    own_normed = lax.dynamic_slice_in_dim(normed, feature_start, local_width, 2)
    input_grad = (
        cotangent.astype(jnp.float32)
        + inverse * (scattered - row_sums[0][..., None] - own_normed * row_sums[1][..., None])
    ).astype(jnp.bfloat16)
    return (
        block_output,
        input_grad,
        wide_sums[0],
        wide_sums[1],
        wide_sums[2],
        wide_sums[3],
        sum_pair(triple_share, "ctx"),
        triple_bias_out,
        sum_pair(mixer_share, "ctx"),
        wide_sums[4],
        sum_pair(widen_share, "ctx"),
        widen_bias_out,
        sum_pair(narrow_share, "ctx"),
    )


def solution(mesh):
    in_specs = (
        P("fsdp", "ctx", "tp"),
        P("fsdp", "ctx"),
        P("fsdp"),
        P("fsdp"),
        P("fsdp"),
        P("fsdp"),
        P("fsdp", None, "tp"),
        P(None, "tp", "fsdp"),
        P("tp", "fsdp"),
        P("fsdp"),
        P("fsdp", "tp"),
        P("tp", "fsdp"),
        P("tp", "fsdp"),
        P("fsdp", "ctx", "tp"),
    )
    out_specs = (
        P("fsdp", "ctx", "tp"),
        P("fsdp", "ctx", "tp"),
        P("fsdp"),
        P("fsdp"),
        P("fsdp"),
        P("fsdp"),
        P("fsdp", None, "tp"),
        P(None, "tp", "fsdp"),
        P("tp", "fsdp"),
        P("fsdp"),
        P("fsdp", "tp"),
        P("tp", "fsdp"),
        P("tp", "fsdp"),
    )
    return jax.shard_map(shards, mesh=mesh, in_specs=in_specs, out_specs=out_specs, check_vma=False)
```
